128 devices in a mesh: seq: 32 (over x_lo, y, z), head: 4 (over x_hi, core).
Axes of the slice: x: 4 (x_hi: 2, x_lo: 2; x = x_hi * 2 + x_lo), y: 4, z: 4, core: 2. Of those that a mesh axis runs over, the one named last changes fastest.
Arguments:
- tokens: bfloat16 [32768, 2048], P('seq'), may hold values from -26 to 26, as said below
- w_query: bfloat16 [2048, 2048], P(None, 'head'), as said below
- w_key: bfloat16 [2048, 2048], P(None, 'head'), as said below
- w_value: bfloat16 [2048, 2048], P(None, 'head'), may hold values from -0.125 to 0.125
- w_out: bfloat16 [2048, 2048], P('head'), may hold values from -0.125 to 0.125
- window_blocks: int32 [256, 3], P('seq'), may hold values from 0 to 255, as said below
- random_blocks: int32 [256, 4], replicated, may hold values from 0 to 255, as said below
- summary_blocks: int32 [256, 2], P('seq'), may hold values from 0 to 3
- seg_start: int32 [512], replicated, may hold values from 0 to 32767, as said below
- seg_end: int32 [512], replicated, may hold values from 1 to 32768, as said below
Outputs:
- mixed: bfloat16 [32768, 2048], P('seq', 'head')
The draws below stay inside these ranges and needn't reach their ends.
Inputs may be any that keep to these rules, and one draw needn't show every extreme that they name: `tokens`: finite activations. `w_query`: a projection scaled by its fan-in. `w_key`: a projection scaled by its fan-in. `window_blocks`: row i names block i first, then two other blocks at most 2 blocks away from i. `random_blocks`: in the rows of one index of seq (aligned runs of 8 rows), the blocks held by any one index of seq are named at most 2 times, and those of some index exactly 2 times. `seg_start`: each segment holds 1 to 512 tokens, segment 0 exactly 512; segment s lies within the tokens of one index of seq, namely index (s // 16 + 16) mod 32. seg_end is greater than seg_start and at most seg_start + 512.
All inputs are finite; a program needn't handle non-finite values.
Results may differ from the reference program's by a relative error of at most 0.0095.
Values may be sent and summed in bfloat16 or wider, within the bound.
A program may use at most 192 MiB of HBM per device.

```python
import jax
import jax.numpy as jnp
from jax import lax

D = 2048
H = 16
HD = 128
BLK = 128
NB_DEV = 8
R = 4
FIXL = 2
NSB = 4
MAXSEG = 512
S_DEV = 1024
TOKENS = 32768
NBLOCKS = 256
NSUM = 512
CAP = 2
N_HEAD = 4


def draw_tokens(key, part):
    base_draw = jnp.clip(jax.random.normal(jax.random.fold_in(key, 1), (TOKENS, D), jnp.float32), -6.0, 6.0)
    return base_draw.astype(jnp.bfloat16)


def query_base(key):
    return jnp.clip(jax.random.normal(jax.random.fold_in(key, 11), (D, H * HD), jnp.float32), -6.0, 6.0) * D ** (-0.5)


def draw_w_query(key, part):
    return query_base(key).astype(jnp.bfloat16)


def draw_w_key(key, part):
    own_part = jnp.clip(jax.random.normal(jax.random.fold_in(key, 12), (D, H * HD), jnp.float32), -6.0, 6.0) * D ** (-0.5)
    return own_part.astype(jnp.bfloat16)


def draw_window_blocks(key, part):
    block_ids = jnp.arange(NBLOCKS, dtype=jnp.int32)
    offsets = jnp.array([-2, -1, 1, 2], jnp.int32)
    target = block_ids[:, None] + offsets[None, :]
    usable = ((target >= 0) & (target < NBLOCKS)).astype(jnp.int32)
    priority = jax.random.randint(key, (NBLOCKS, 4), 0, 1024) * 4 + jnp.arange(4, dtype=jnp.int32)[None, :] + usable * 8192
    ordering = jnp.argsort(-priority, axis=1)
    picked = jnp.take_along_axis(target, ordering[:, :2], axis=1)
    return jnp.concatenate([block_ids[:, None], picked], axis=1).astype(jnp.int32)


def owners_of(key):
    devices = NBLOCKS // NB_DEV
    ref_count = NB_DEV * R

    def one_device(dev_key):
        first_owner = jax.random.randint(jax.random.fold_in(dev_key, 1), (), 0, devices)
        shuffled = jax.random.permutation(jax.random.fold_in(dev_key, 2), (devices - 1) * CAP)
        others = shuffled // CAP
        others = others + (others >= first_owner).astype(jnp.int32)
        chosen = jnp.concatenate([jnp.full((CAP,), first_owner, jnp.int32), others[:ref_count - CAP].astype(jnp.int32)])
        return jax.random.permutation(jax.random.fold_in(dev_key, 3), chosen)
    key_list = jax.random.split(key, devices)
    return jax.vmap(one_device)(key_list)


def draw_random_blocks(key, part):
    owners = owners_of(jax.random.fold_in(key, 31))
    local_ids = jax.random.randint(jax.random.fold_in(key, 32), owners.shape, 0, NB_DEV)
    return (owners * NB_DEV + local_ids).reshape(NBLOCKS, R).astype(jnp.int32)


def segment_pair(key):
    devices = NBLOCKS // NB_DEV
    share_rows = NSUM // devices
    row_ids = jnp.arange(NSUM, dtype=jnp.int32)
    home = (row_ids // share_rows + devices // 2) % devices
    raw = jax.random.randint(jax.random.fold_in(key, 2), (NSUM,), 0, MAXSEG)
    span_rows = 1 + raw * raw // MAXSEG
    span_rows = jnp.where(row_ids == 0, MAXSEG, span_rows).astype(jnp.int32)
    draw_offset = jax.random.randint(jax.random.fold_in(key, 1), (NSUM,), 0, S_DEV + 1)
    room = S_DEV - span_rows + 1
    offset_rows = draw_offset % room
    start_rows = home * S_DEV + offset_rows
    return (start_rows.astype(jnp.int32), (start_rows + span_rows).astype(jnp.int32))


def draw_seg_start(key, part):
    return segment_pair(jax.random.fold_in(key, 41))[0]


def draw_seg_end(key, part):
    return segment_pair(jax.random.fold_in(key, 41))[1]


def plant(entries, own_key, least, high):
    longest = entries.shape.index(max(entries.shape))
    spots = []
    for shift in (0, 1):
        where = [jax.random.randint(jax.random.fold_in(own_key, axis), (), 0, length) for axis, length in enumerate(entries.shape)]
        where[longest] = (where[longest] + shift) % entries.shape[longest]
        spots.append(tuple(where))
    return entries.at[spots[0]].set(least).at[spots[1]].set(high)


def levels(own_key, extent, cuts, least, largest):
    def one(axis_at, blocks):
        draws = jax.random.uniform(jax.random.fold_in(jax.random.fold_in(own_key, 6), axis_at), (blocks,), jnp.float32, least / len(cuts), largest / len(cuts))
        return jnp.repeat(jnp.exp(draws), extent[axis_at] // blocks).reshape((-1,) + (1,) * (len(extent) - axis_at - 1))

    gain = one(*cuts[0])
    for cut in cuts[1:]:
        gain = gain * one(*cut)
    return gain


def bell_draw(own_key, extent, scale, reach, cuts=(), kind=jnp.bfloat16):
    values = scale * jax.random.normal(own_key, extent, jnp.float32)
    if cuts:
        values = values * levels(own_key, extent, cuts, -0.22, 0.18)
    return jnp.clip(values, -reach, reach).astype(kind)


def setup_inputs(seed: int = 0) -> dict:
    seeds = jax.random.split(jax.random.key(seed), 11)
    tokens = draw_tokens(jax.random.fold_in(seeds[10], 71), 0)
    w_query = draw_w_query(jax.random.fold_in(seeds[10], 71), 0)
    w_key = draw_w_key(jax.random.fold_in(seeds[10], 71), 0)
    w_value = bell_draw(seeds[3], (D, H * HD), D ** -0.5, 0.125, ((1, 4),))
    w_out = bell_draw(seeds[4], (H * HD, D), (H * HD) ** -0.5, 0.125, ((0, 4),))
    window_blocks = draw_window_blocks(jax.random.fold_in(seeds[10], 71), 0)
    random_blocks = draw_random_blocks(jax.random.fold_in(seeds[10], 71), 0)
    summary_blocks = plant(jax.random.randint(seeds[7], (NBLOCKS, FIXL), 0, NSB), jax.random.fold_in(seeds[7], 1), 0, NSB - 1).astype(jnp.int32)
    seg_start = draw_seg_start(jax.random.fold_in(seeds[10], 71), 0)
    seg_end = draw_seg_end(jax.random.fold_in(seeds[10], 71), 0)
    return {"tokens": tokens, "w_query": w_query, "w_key": w_key, "w_value": w_value, "w_out": w_out, "window_blocks": window_blocks, "random_blocks": random_blocks, "summary_blocks": summary_blocks, "seg_start": seg_start, "seg_end": seg_end}


def project(tokens, weight):
    return jnp.dot(tokens, weight, preferred_element_type=jnp.float32).astype(jnp.bfloat16)


def reference(tokens, w_query, w_key, w_value, w_out, window_blocks, random_blocks, summary_blocks, seg_start, seg_end):
    columns = H * HD
    queries = project(tokens, w_query)
    key_rows = project(tokens, w_key)
    values = project(tokens, w_value)
    key_value = jnp.concatenate([key_rows, values], axis=1)
    padded_rows = jnp.concatenate([key_value, jnp.zeros((MAXSEG, 2 * columns), key_value.dtype)], axis=0)

    def pool(inputs):
        first_row, last_row = inputs
        window = lax.dynamic_slice_in_dim(padded_rows, first_row.astype(jnp.int32), MAXSEG, 0).astype(jnp.float32)
        inside = ((first_row.astype(jnp.int32) + jnp.arange(MAXSEG, dtype=jnp.int32)) < last_row.astype(jnp.int32)).astype(jnp.float32)
        counts = (last_row - first_row).astype(jnp.float32)
        return jnp.sum(window * inside[:, None], axis=0) / counts

    summary = lax.map(pool, (seg_start, seg_end)).astype(jnp.bfloat16).reshape(NSB, BLK, 2, columns)
    blocks = key_value.reshape(NBLOCKS, BLK, 2, columns)
    score_scale = HD ** -0.5

    def attend(inputs):
        block_queries, window_ids, random_ids, summary_ids = inputs
        gathered = jnp.concatenate([blocks[window_ids], blocks[random_ids], summary[summary_ids]], axis=0)
        gathered = gathered.reshape(-1, 2, H, HD).astype(jnp.float32)
        lifted = block_queries.reshape(BLK, H, HD).astype(jnp.float32)
        scores = jnp.einsum("qhd,khd->hqk", lifted, gathered[:, 0], precision=lax.Precision.HIGHEST) * score_scale
        row_peak = jnp.max(scores, axis=-1, keepdims=True)
        weights = jnp.exp(scores - row_peak)
        row_total = jnp.sum(weights, axis=-1)
        rounded = lax.optimization_barrier(weights.astype(jnp.bfloat16)).astype(jnp.float32)
        mixed = jnp.einsum("hqk,khd->qhd", rounded, gathered[:, 1], precision=lax.Precision.HIGHEST)
        mixed = mixed / jnp.transpose(row_total)[:, :, None]
        return mixed.reshape(BLK, columns).astype(jnp.bfloat16)

    attended = lax.map(attend, (queries.reshape(NBLOCKS, BLK, columns), window_blocks, random_blocks, summary_blocks))
    attended = attended.reshape(TOKENS, columns)
    group_cols = columns // N_HEAD
    out_sum = jnp.zeros((TOKENS, D), jnp.float32)
    for group_idx in range(N_HEAD):
        lower = group_idx * group_cols
        partial_value = jnp.dot(attended[:, lower:lower + group_cols], w_out[lower:lower + group_cols], preferred_element_type=jnp.float32)
        out_sum = out_sum + lax.optimization_barrier(partial_value.astype(jnp.bfloat16)).astype(jnp.float32)
    return out_sum.astype(jnp.bfloat16)
```

```python
import functools

import jax
import jax.numpy as jnp
from jax import lax
from jax.experimental import pallas as pl
from jax.experimental.pallas import tpu as pltpu
from jax.sharding import PartitionSpec as P

HD = 128
BLK = 128
ROWS = 1024
SUMS = 16
SLAB = ROWS + SUMS
LISTS = 9
MESH = pl.DeviceIdType.MESH
ORDER = (0, 1, 3, 2)
ANY = pl.BlockSpec(memory_space=pl.ANY)
VMEM = pl.BlockSpec(memory_space=pltpu.VMEM)
SMEM = pl.BlockSpec(memory_space=pltpu.SMEM)


def place():
    seq = lax.axis_index("seq")
    head = lax.axis_index("head")
    return seq // 16, (seq // 4) % 4, seq % 4, head // 2, head % 2


def device(xl, y, z, xh, c):
    return (xl * 16 + y * 4 + z, xh * 2 + c)


def project_kernel(
    tok_hbm, wk_hbm, wv_hbm, wq_hbm, first_ref, last_ref, kv_ref, q_ref, tok, w, tok_sem, w_sem
):
    parts = 4
    step = ROWS // parts
    weights = (wk_hbm, wv_hbm, wq_hbm)
    tok_copies = [
        pltpu.make_async_copy(
            tok_hbm.at[pl.ds(r * step, step)], tok.at[pl.ds(r * step, step)], tok_sem.at[r]
        )
        for r in range(parts)
    ]
    w_copies = [pltpu.make_async_copy(weights[t], w.at[t], w_sem.at[t]) for t in range(3)]
    w_copies[0].start()
    for copy in tok_copies:
        copy.start()
    w_copies[1].start()
    w_copies[2].start()
    position = lax.broadcasted_iota(jnp.int32, (SUMS, ROWS), 1)
    first = first_ref[...]
    last = last_ref[...]
    member = ((position >= first) & (position < last)).astype(jnp.float32).astype(jnp.bfloat16)
    counts = (last - first).astype(jnp.float32)
    for t in range(3):
        w_copies[t].wait()
        for r in range(parts):
            if t == 0:
                tok_copies[r].wait()
            rows = pl.ds(r * step, step)
            out = jnp.dot(tok[rows], w[t], preferred_element_type=jnp.float32).astype(jnp.bfloat16)
            for j in range(4):
                piece = out[:, j * HD : (j + 1) * HD]
                if t < 2:
                    kv_ref[j, t, rows] = piece
                else:
                    q_ref[j, rows] = piece
        if t < 2:
            for j in range(4):
                sums = jnp.dot(
                    member, kv_ref[j, t, pl.ds(0, ROWS)], preferred_element_type=jnp.float32
                )
                kv_ref[j, t, pl.ds(ROWS, SUMS)] = (sums / counts).astype(jnp.bfloat16)


def project(tokens, w_key, w_value, w_query, first, last):
    return pl.pallas_call(
        project_kernel,
        out_shape=(
            jax.ShapeDtypeStruct((4, 2, SLAB, HD), jnp.bfloat16),
            jax.ShapeDtypeStruct((4, ROWS, HD), jnp.bfloat16),
        ),
        in_specs=[ANY] * 4 + [VMEM] * 2,
        out_specs=(VMEM, VMEM),
        scratch_shapes=[
            pltpu.VMEM(tokens.shape, jnp.bfloat16),
            pltpu.VMEM((3, *w_key.shape), jnp.bfloat16),
            pltpu.SemaphoreType.DMA((4,)),
            pltpu.SemaphoreType.DMA((3,)),
        ],
        name="project",
    )(tokens, w_key, w_value, w_query, first, last)


def spread_kernel(
    kv_ref, q_ref, list_ref, wo_ref,
    kvall_ref, qall_ref, lists_ref, wcols_ref,
    stage,
    in_send, in_recv, q_send, q_recv, l_send, l_recv, w_send, w_recv,
    up_send, up_recv, down_send, down_recv, upk_send, upk_recv, downv_send, downv_recv,
    core_send, core_recv, local_sem,
):
    xl, y, z, xh, c = place()
    seq = lax.axis_index("seq")
    head = lax.axis_index("head")
    above, below = (z + 1) % 4, (z + 3) % 4
    across = (z + 2) % 4
    mine = xl == c
    up_dev = device(xl, y, above, xh, c)
    down_dev = device(xl, y, below, xh, c)
    twin = device(xl, y, z, xh, 1 - c)

    def partner(d):
        return device(c, (y + d) % 4, z, xh, xl)

    barrier = pltpu.get_barrier_semaphore()

    def greet(target):
        pl.semaphore_signal(barrier, inc=1, device_id=target, device_id_type=MESH)

    for d in (1, 2, 3):
        greet(partner(d))
        greet((seq, (head + d) % 4))
    greet(up_dev)
    greet(down_dev)

    @pl.when(jnp.logical_not(mine))
    def _():
        greet(partner(0))

    pl.semaphore_wait(barrier, 8 + (xl + c) % 2)

    def remote(src, dst, send, recv, target):
        return pltpu.make_async_remote_copy(
            src_ref=src, dst_ref=dst, send_sem=send, recv_sem=recv,
            device_id=target, device_id_type=MESH,
        )

    def kv_in(d):
        j = (y + d) % 4
        return remote(kv_ref.at[j], kvall_ref.at[seq], in_send.at[d], in_recv.at[y], partner(d))

    def q_in(d):
        j = (y + d) % 4
        return remote(q_ref.at[j], qall_ref.at[y], q_send.at[d], q_recv.at[y], partner(d))

    def l_in(d):
        return remote(list_ref, lists_ref.at[y], l_send.at[d], l_recv.at[y], partner(d))

    def w_in(k):
        target = (head + k) % 4
        columns = pl.ds(pl.multiple_of(target * 512, 512), 512)
        return remote(
            wo_ref.at[:, columns], wcols_ref.at[head], w_send.at[k - 1], w_recv.at[k - 1],
            (seq, target),
        )

    stage_in = pltpu.make_async_copy(kv_ref.at[y], stage, local_sem.at[0])
    stage_out = pltpu.make_async_copy(stage, kvall_ref.at[seq], local_sem.at[0])
    q_local = pltpu.make_async_copy(q_ref.at[y], qall_ref.at[y], local_sem.at[1])
    l_local = pltpu.make_async_copy(list_ref, lists_ref.at[y], local_sem.at[2])
    w_local = pltpu.make_async_copy(
        wo_ref.at[:, pl.ds(pl.multiple_of(head * 512, 512), 512)], wcols_ref.at[head],
        local_sem.at[3],
    )

    @pl.when(mine)
    def _():
        stage_in.start()

    @pl.when(jnp.logical_not(mine))
    def _():
        kv_in(0).start()

    for d in ORDER[1:]:
        kv_in(d).start()

    @pl.when(mine)
    def _():
        stage_in.wait()
        stage_out.start()

    @pl.when(jnp.logical_not(mine))
    def _():
        q_in(0).start()
        l_in(0).start()

    for d in ORDER[1:]:
        q_in(d).start()
        l_in(d).start()
    w_local.start()
    for k in (2, 1, 3):
        w_in(k).start()

    def row(yy, zz):
        return c * 16 + yy * 4 + zz

    def up_own(yy, s):
        return remote(kvall_ref.at[s], kvall_ref.at[s], up_send.at[yy], up_recv.at[yy], up_dev)

    def down_own(yy, s):
        return remote(
            kvall_ref.at[s], kvall_ref.at[s], down_send.at[yy], down_recv.at[yy], down_dev
        )

    def up_relay(yy, s):
        return remote(
            kvall_ref.at[s, 0], kvall_ref.at[s, 0], upk_send.at[yy], upk_recv.at[yy], up_dev
        )

    def down_relay(yy, s):
        return remote(
            kvall_ref.at[s, 1], kvall_ref.at[s, 1], downv_send.at[yy], downv_recv.at[yy], down_dev
        )

    def to_twin(yy, k, s):
        return remote(
            kvall_ref.at[s], kvall_ref.at[s], core_send.at[yy, k], core_recv.at[yy, k], twin
        )

    for step in range(6):
        if step < 4:
            d = ORDER[step]
            yy = (y + d) % 4
            s = row(yy, z)
            arrived = remote(
                kv_ref.at[0], kvall_ref.at[s], in_send.at[d], in_recv.at[yy], partner(d)
            )
            if d == 0:

                @pl.when(mine)
                def _():
                    stage_out.wait()

                @pl.when(jnp.logical_not(mine))
                def _():
                    arrived.wait_recv()

            else:
                arrived.wait_recv()
            up_own(yy, s).start()
            down_own(yy, s).start()
            to_twin(yy, 0, s).start()
        if 1 <= step < 5:
            yy = (y + ORDER[step - 1]) % 4
            s = row(yy, below)
            up_own(yy, s).wait_recv()
            up_relay(yy, s).start()
            to_twin(yy, 1, s).start()
            s = row(yy, above)
            down_own(yy, s).wait_recv()
            down_relay(yy, s).start()
            to_twin(yy, 2, s).start()
        if 2 <= step:
            yy = (y + ORDER[step - 2]) % 4
            s = row(yy, across)
            up_relay(yy, s).wait_recv()
            down_relay(yy, s).wait_recv()
            to_twin(yy, 3, s).start()

    for d in ORDER:
        j = (y + d) % 4

        def finish():
            kv_in(d).wait_send()
            q_in(d).wait_send()
            l_in(d).wait_send()
            remote(
                q_ref.at[0], qall_ref.at[j], q_send.at[d], q_recv.at[j], partner(d)
            ).wait_recv()
            remote(
                list_ref, lists_ref.at[j], l_send.at[d], l_recv.at[j], partner(d)
            ).wait_recv()

        if d == 0:

            @pl.when(jnp.logical_not(mine))
            def _():
                finish()

            @pl.when(mine)
            def _():
                q_local.start()
                l_local.start()
                q_local.wait()
                l_local.wait()

        else:
            finish()
    w_local.wait()
    for k in (1, 2, 3):
        w_in(k).wait_send()
        source = (head + 4 - k) % 4
        remote(
            wo_ref.at[:, pl.ds(0, 512)], wcols_ref.at[source], w_send.at[k - 1],
            w_recv.at[k - 1], (seq, source),
        ).wait_recv()
    for i in range(4):
        yy = (y + ORDER[i]) % 4
        up_own(yy, row(yy, z)).wait_send()
        down_own(yy, row(yy, z)).wait_send()
        up_relay(yy, row(yy, below)).wait_send()
        down_relay(yy, row(yy, above)).wait_send()
        for k, zz in enumerate((z, below, above, across)):
            to_twin(yy, k, row(yy, zz)).wait_send()
            to_twin(yy, k, (1 - c) * 16 + yy * 4 + zz).wait_recv()


def spread(kv, q, lists, w_out):
    four = pltpu.SemaphoreType.DMA((4,))
    grid4 = pltpu.SemaphoreType.DMA((4, 4))
    return pl.pallas_call(
        spread_kernel,
        out_shape=(
            jax.ShapeDtypeStruct((32, 2, SLAB, HD), jnp.bfloat16),
            jax.ShapeDtypeStruct((4, ROWS, HD), jnp.bfloat16),
            jax.ShapeDtypeStruct((4, 8, 128), jnp.int32),
            jax.ShapeDtypeStruct((4, 512, 512), jnp.bfloat16),
        ),
        in_specs=[ANY] * 4,
        out_specs=(ANY,) * 4,
        scratch_shapes=[pltpu.VMEM((2, SLAB, HD), jnp.bfloat16)]
        + [four] * 16
        + [grid4, grid4, four],
        compiler_params=pltpu.CompilerParams(collective_id=0, has_side_effects=True),
        name="spread",
    )(kv, q, lists, w_out)


def attend_kernel(lists_ref, kv_ref, q_ref, o_ref, sums):
    for t in range(32):
        home = (t + 16) % 32
        for k in range(2):
            sums[k, t // 8, pl.ds((t % 8) * SUMS, SUMS)] = kv_ref[home, k, pl.ds(ROWS, SUMS)]
    factor = HD ** (-0.5) * 1.4426950408889634

    def block(i, carry):
        run = i // 8
        within = i % 8
        rows = pl.ds(pl.multiple_of(within * BLK, BLK), BLK)
        query = q_ref[run, rows]
        keys, vals = [], []
        for n in range(LISTS):
            b = lists_ref[run, within, n]
            if n < LISTS - 2:
                span = pl.ds(pl.multiple_of((b % 8) * BLK, BLK), BLK)
                keys.append(kv_ref[b // 8, 0, span])
                vals.append(kv_ref[b // 8, 1, span])
            else:
                keys.append(sums[0, b])
                vals.append(sums[1, b])
        key = jnp.concatenate(keys, axis=0)
        val = jnp.concatenate(vals, axis=0)
        scores = lax.dot_general(
            query, key, (((1,), (1,)), ((), ())), preferred_element_type=jnp.float32
        )
        peak = jnp.max(scores, axis=1, keepdims=True)
        weights = jnp.exp2((scores - peak) * factor)
        total = jnp.sum(weights, axis=1, keepdims=True)
        out = jnp.dot(weights.astype(jnp.bfloat16), val, preferred_element_type=jnp.float32)
        o_ref[run, rows] = (out / total).astype(jnp.bfloat16)
        return carry

    lax.fori_loop(0, 32, block, 0, unroll=2)


def attend(lists, kv, q):
    return pl.pallas_call(
        attend_kernel,
        out_shape=jax.ShapeDtypeStruct((4, ROWS, HD), jnp.bfloat16),
        in_specs=[SMEM, VMEM, VMEM],
        out_specs=VMEM,
        scratch_shapes=[pltpu.VMEM((2, 4, BLK, HD), jnp.bfloat16)],
        name="attend",
    )(lists, kv, q)


def collect_kernel(o_ref, all_ref, send, recv, core_send, core_recv, local_sem):
    xl, y, z, xh, c = place()
    mine = xl == c
    twin = device(xl, y, z, xh, 1 - c)

    def partner(d, e):
        return device(c, (y + d) % 4, z, (xh + e) % 2, xl)

    barrier = pltpu.get_barrier_semaphore()

    def greet(target):
        pl.semaphore_signal(barrier, inc=1, device_id=target, device_id_type=MESH)

    greet(twin)
    for d in range(4):
        greet(partner(d, 1))
        if d > 0:
            greet(partner(d, 0))

    @pl.when(jnp.logical_not(mine))
    def _():
        greet(partner(0, 0))

    pl.semaphore_wait(barrier, 8 + (xl + c) % 2)

    def remote(src, dst, send, recv, target):
        return pltpu.make_async_remote_copy(
            src_ref=src, dst_ref=dst, send_sem=send, recv_sem=recv,
            device_id=target, device_id_type=MESH,
        )

    my_head = (xh * 2 + xl) * 4 + y

    def out(d, e):
        return remote(
            o_ref.at[(y + d) % 4], all_ref.at[my_head], send.at[d, e], recv.at[y, e],
            partner(d, e),
        )

    local = pltpu.make_async_copy(o_ref.at[y], all_ref.at[my_head], local_sem)

    @pl.when(mine)
    def _():
        local.start()

    for d in (2, 1, 3, 0):
        out(d, 1).start()
        if d > 0:
            out(d, 0).start()
        else:

            @pl.when(jnp.logical_not(mine))
            def _():
                out(0, 0).start()

    def to_twin(yy, e, h):
        return remote(
            all_ref.at[h], all_ref.at[h], core_send.at[yy, e], core_recv.at[yy, e], twin
        )

    for d in ORDER:
        yy = (y + d) % 4
        for e in (0, 1):
            h = (((xh + e) % 2) * 2 + c) * 4 + yy
            arrived = remote(
                o_ref.at[0], all_ref.at[h], send.at[d, e], recv.at[yy, e], partner(d, e)
            )
            if d == 0 and e == 0:

                @pl.when(mine)
                def _():
                    local.wait()

                @pl.when(jnp.logical_not(mine))
                def _():
                    arrived.wait_recv()

            else:
                arrived.wait_recv()
            to_twin(yy, e, h).start()
    for d in ORDER:
        yy = (y + d) % 4
        for e in (0, 1):
            if d == 0 and e == 0:

                @pl.when(jnp.logical_not(mine))
                def _():
                    out(0, 0).wait_send()

            else:
                out(d, e).wait_send()
            h = (((xh + e) % 2) * 2 + c) * 4 + yy
            to_twin(yy, e, h).wait_send()
            other = (((xh + e) % 2) * 2 + 1 - c) * 4 + yy
            to_twin(yy, e, other).wait_recv()


def collect(attended):
    return pl.pallas_call(
        collect_kernel,
        out_shape=jax.ShapeDtypeStruct((16, ROWS, HD), jnp.bfloat16),
        in_specs=[ANY],
        out_specs=ANY,
        scratch_shapes=[
            pltpu.SemaphoreType.DMA((4, 2)),
            pltpu.SemaphoreType.DMA((4, 2)),
            pltpu.SemaphoreType.DMA((4, 2)),
            pltpu.SemaphoreType.DMA((4, 2)),
            pltpu.SemaphoreType.DMA,
        ],
        compiler_params=pltpu.CompilerParams(collective_id=1, has_side_effects=True),
        name="collect",
    )(attended)


def mix_kernel(a_ref, w_ref, o_ref):
    rows = jnp.concatenate([a_ref[h] for h in range(16)], axis=1)
    o_ref[...] = jnp.dot(rows, w_ref[...], preferred_element_type=jnp.float32).astype(jnp.bfloat16)


def mix(attended, w_cols):
    step = 256
    return pl.pallas_call(
        mix_kernel,
        grid=(ROWS // step,),
        out_shape=jax.ShapeDtypeStruct((ROWS, 512), jnp.bfloat16),
        in_specs=[
            pl.BlockSpec((16, step, HD), lambda i: (0, i, 0)),
            pl.BlockSpec((2048, 512), lambda i: (0, 0), pipeline_mode=pl.Buffered(1)),
        ],
        out_specs=pl.BlockSpec((step, 512), lambda i: (i, 0)),
        name="mix",
    )(attended, w_cols)


def per_device(
    tokens, w_query, w_key, w_value, w_out,
    window_blocks, random_blocks, summary_blocks, seg_start, seg_end,
):
    seq = lax.axis_index("seq")
    own = ((seq + 16) % 32) * SUMS
    first = lax.dynamic_slice_in_dim(seg_start, own, SUMS)[:, None] - seq * ROWS
    last = lax.dynamic_slice_in_dim(seg_end, own, SUMS)[:, None] - seq * ROWS
    random_own = lax.dynamic_slice_in_dim(random_blocks, seq * 8, 8)
    lists = jnp.concatenate([window_blocks, random_own, summary_blocks], axis=1)
    lists = jnp.pad(lists, ((0, 0), (0, 128 - LISTS)))
    kv, q = project(tokens, w_key, w_value, w_query, first, last)
    kvall, qall, lists_all, w_cols = spread(kv, q, lists, w_out)
    attended = attend(lists_all, kvall, qall)
    everything = collect(attended)
    return mix(everything, w_cols.reshape(2048, 512))


def solution(mesh):
    placed = (
        P("seq", None),
        P(None, "head"),
        P(None, "head"),
        P(None, "head"),
        P("head", None),
        P("seq", None),
        P(),
        P("seq", None),
        P(),
        P(),
    )
    return jax.shard_map(
        per_device, mesh=mesh, in_specs=placed, out_specs=P("seq", "head"), check_vma=False
    )
```
